1024 devices in a mesh: sect: 16 (over z), tx: 16 (over x_hi, y), ty: 4 (over x_lo, core).
Axes of the slice: x: 4 (x_hi: 2, x_lo: 2; x = x_hi * 2 + x_lo), y: 8, z: 16, core: 2. Of those that a mesh axis runs over, the one named last changes fastest.
Arguments:
- solute_amounts: float32 [19, 16, 32, 8192], P(None, None, 'sect', ('tx', 'ty')), may hold values from 0.2 to 2
- submerged_layer_tally: int32 [32, 8192], P('sect', ('tx', 'ty')), may hold values from 0 to 16
- zonal_boundary_transport: float32 [16, 32, 8192], P('sect', None, ('tx', 'ty')), may hold values from -0.25 to 0.25
- meridional_boundary_transport: float32 [16, 32, 8192], P('sect', None, ('tx', 'ty')), may hold values from -0.25 to 0.25
- diffusion_factor: float32 [16, 32, 8192], P('sect', None, ('tx', 'ty')), may hold values from 0.05 to 5
- thermal_state: float32 [16, 32, 8192], P('sect', None, ('tx', 'ty')), may hold values from -2 to 30
- saltiness_field: float32 [16, 32, 8192], P('sect', None, ('tx', 'ty')), may hold values from 32 to 38
- chemistry_matrix: float32 [19, 19], replicated, may hold values from -1.25 to 1.25
Outputs:
- advanced_solutes: float32 [19, 16, 32, 8192], P(None, None, 'sect', ('tx', 'ty'))
- heating: float32 [16, 32, 8192], P('sect', None, ('tx', 'ty'))
The draws below stay inside these ranges and needn't reach their ends.
All inputs are finite; a program needn't handle non-finite values.
Results may differ from the reference program's by a relative error of at most 0.0003.
Values sent between devices are 32-bit elements; how exact they have to be, the bound alone decides.
No kernel may reach another device: no remote copies, remote signals or barrier semaphores. Data moves between devices by JAX's collectives and lax.ppermute only.
A program may use at most 32 MiB of HBM per device.

```python
import math
import jax
import jax.numpy as jnp
from jax import lax

NTR = 19
STRATA_TOTAL = 16
ZONAL_SIZE = 32
MERIDIONAL_SIZE = 8192


def set_ends(values, own_key, least, high):
    place = [jax.random.randint(jax.random.fold_in(own_key, axis), (), 0, length) for axis, length in enumerate(values.shape)]
    widest = values.shape.index(max(values.shape))
    beside = place[:widest] + [(place[widest] + 1) % values.shape[widest]] + place[widest + 1:]
    return values.at[tuple(place)].set(least).at[tuple(beside)].set(high)


def levels(own_key, dims, shards, low, top_value):
    def one(dim, blocks):
        draws = jax.random.uniform(jax.random.fold_in(jax.random.fold_in(own_key, 6), dim), (blocks,), jnp.float32, low / len(shards), top_value / len(shards))
        return jnp.repeat(jnp.exp(draws), dims[dim] // blocks).reshape((-1,) + (1,) * (len(dims) - dim - 1))

    level = one(*shards[0])
    for cut in shards[1:]:
        level = level * one(*cut)
    return level


def noise(stream_key, extent, width, most, kind=jnp.bfloat16):
    entries = jax.random.normal(stream_key, extent, jnp.float32) * width
    return jnp.minimum(jnp.maximum(entries, -most), most).astype(kind)


def setup_inputs(seed: int = 0) -> dict:
    keys = jax.random.split(jax.random.key(seed), 9)
    solute_amounts = jnp.clip(jnp.exp(math.log(2.0) - 2.3025851 * jax.random.uniform(keys[0], (NTR, STRATA_TOTAL, ZONAL_SIZE, MERIDIONAL_SIZE), jnp.float32) ** levels(keys[0], (NTR, STRATA_TOTAL, ZONAL_SIZE, MERIDIONAL_SIZE), ((2, 16), (3, 64)), -0.2, 0.2)), 0.2, 2.0)
    submerged_layer_tally = set_ends(jax.random.randint(keys[1], (ZONAL_SIZE, MERIDIONAL_SIZE), 0, STRATA_TOTAL + 1), jax.random.fold_in(keys[1], 1), 0, STRATA_TOTAL).astype(jnp.int32)
    zonal_boundary_transport = jnp.clip(jax.random.uniform(keys[2], (STRATA_TOTAL, ZONAL_SIZE, MERIDIONAL_SIZE), jnp.float32, -0.25, 0.25) * levels(keys[2], (STRATA_TOTAL, ZONAL_SIZE, MERIDIONAL_SIZE), ((0, 16), (2, 64)), -0.4, 0.0), -0.25, 0.25)
    meridional_boundary_transport = jnp.clip(jax.random.uniform(keys[3], (STRATA_TOTAL, ZONAL_SIZE, MERIDIONAL_SIZE), jnp.float32, -0.25, 0.25) * levels(keys[3], (STRATA_TOTAL, ZONAL_SIZE, MERIDIONAL_SIZE), ((0, 16), (2, 64)), -0.4, 0.0), -0.25, 0.25)
    diffusion_factor = jnp.clip(jnp.exp(math.log(5.0) - 4.6051702 * jax.random.uniform(keys[4], (STRATA_TOTAL, ZONAL_SIZE, MERIDIONAL_SIZE), jnp.float32) ** levels(keys[4], (STRATA_TOTAL, ZONAL_SIZE, MERIDIONAL_SIZE), ((0, 16), (2, 64)), -0.2, 0.2)), 0.05, 5.0)
    thermal_state = jnp.clip(-2.0 + 32.0 * jax.random.uniform(keys[5], (STRATA_TOTAL, ZONAL_SIZE, MERIDIONAL_SIZE), jnp.float32) ** levels(keys[5], (STRATA_TOTAL, ZONAL_SIZE, MERIDIONAL_SIZE), ((0, 16), (2, 64)), -0.2, 0.2), -2.0, 30.0)
    saltiness_field = jnp.clip(32.0 + 6.0 * jax.random.uniform(keys[6], (STRATA_TOTAL, ZONAL_SIZE, MERIDIONAL_SIZE), jnp.float32) ** levels(keys[6], (STRATA_TOTAL, ZONAL_SIZE, MERIDIONAL_SIZE), ((0, 16), (2, 64)), -0.2, 0.2), 32.0, 38.0)
    chemistry_matrix = noise(keys[7], (NTR, NTR), NTR ** -0.5, 1.25, jnp.float32)
    return dict(solute_amounts=solute_amounts, submerged_layer_tally=submerged_layer_tally, zonal_boundary_transport=zonal_boundary_transport, meridional_boundary_transport=meridional_boundary_transport, diffusion_factor=diffusion_factor, thermal_state=thermal_state, saltiness_field=saltiness_field, chemistry_matrix=chemistry_matrix)


def window(array, start, length, along):
    return lax.slice_in_dim(array, start, start + length, axis=along)


def minmod(first, second):
    return jnp.where(first * second > 0, jnp.sign(first) * jnp.minimum(jnp.abs(first), jnp.abs(second)), 0.0)


def sweep(values, courant, along, length):
    far_low = window(values, 0, length + 1, along)
    near_low = window(values, 1, length + 1, along)
    near_high = window(values, 2, length + 1, along)
    far_high = window(values, 3, length + 1, along)
    upwind_east = near_low + 0.5 * (1.0 - courant) * minmod(near_low - far_low, near_high - near_low)
    upwind_west = near_high - 0.5 * (1.0 + courant) * minmod(near_high - near_low, far_high - near_high)
    face_flux = courant * jnp.where(courant >= 0, upwind_east, upwind_west)
    return window(face_flux, 0, length, along) - window(face_flux, 1, length, along)


def advect(conc_pad, wet_pad, east_faces, north_faces):
    cells_x = conc_pad.shape[2] - 4
    cells_y = conc_pad.shape[3] - 4
    inner_y = conc_pad[:, :, :, 2:cells_y + 2]
    mask_y = wet_pad[:, :, 2:cells_y + 2]
    open_x = mask_y[:, 1:cells_x + 2] * mask_y[:, 2:cells_x + 3]
    tend_x = sweep(inner_y, east_faces * open_x, 2, cells_x)
    inner_x = conc_pad[:, :, 2:cells_x + 2, :]
    mask_x = wet_pad[:, 2:cells_x + 2, :]
    open_y = mask_x[:, :, 1:cells_y + 2] * mask_x[:, :, 2:cells_y + 3]
    tend_y = sweep(inner_x, north_faces * open_y, 3, cells_y)
    return conc_pad[:, :, 2:cells_x + 2, 2:cells_y + 2] + tend_x + tend_y


def diffuse(moved, diffusion_factor, ocean_indicator):
    lower_mask = jnp.concatenate([ocean_indicator[1:], jnp.zeros_like(ocean_indicator[:1])], 0)
    coupling = diffusion_factor * ocean_indicator * lower_mask
    upper_link = jnp.concatenate([jnp.zeros_like(coupling[:1]), coupling[:-1]], 0)
    diagonal = 1.0 + upper_link + coupling
    source_all = jnp.moveaxis(moved, 1, 0)

    def forward(carry, inputs):
        sweep_ratio, sweep_rhs = carry
        diag_now, upper_now, coupling_now, source = inputs
        divisor = diag_now + upper_now * sweep_ratio
        new_ratio = -coupling_now / divisor
        new_rhs = (source + upper_now[None] * sweep_rhs) / divisor[None]
        return (new_ratio, new_rhs), (new_ratio, new_rhs)

    start = (jnp.zeros(diagonal.shape[1:], jnp.float32), jnp.zeros(source_all.shape[1:], jnp.float32))
    unused, (ratios, rhs_all) = lax.scan(forward, start, (diagonal, upper_link, coupling, source_all))

    def backward(following, inputs):
        sweep_ratio, sweep_rhs = inputs
        solved = sweep_rhs - sweep_ratio[None] * following
        return solved, solved

    unused, solved_all = lax.scan(backward, jnp.zeros(source_all.shape[1:], jnp.float32), (ratios, rhs_all), reverse=True)
    return jnp.moveaxis(solved_all, 0, 1)


def perform_chemistry(blended_solutes, thermal_state, saltiness_field, chemistry_matrix, ocean_indicator):
    expansion_speed = jnp.exp(0.0633 * (thermal_state - 15.0)) * (1.0 + 0.25 * (saltiness_field - 35.0))
    reacted = jnp.einsum("ij,jkxy->ikxy", chemistry_matrix, blended_solutes, precision=lax.Precision.HIGHEST)
    return ocean_indicator[None] * (blended_solutes + 0.2 * expansion_speed[None] * reacted)


def reference(solute_amounts, submerged_layer_tally, zonal_boundary_transport, meridional_boundary_transport, diffusion_factor, thermal_state, saltiness_field, chemistry_matrix):
    depth_index = lax.broadcasted_iota(jnp.int32, zonal_boundary_transport.shape, 0)
    ocean_indicator = (depth_index < submerged_layer_tally[None]).astype(jnp.float32)
    grid_x = zonal_boundary_transport.shape[1]
    grid_y = zonal_boundary_transport.shape[2]
    spread = ((0, 0), (2, 2), (2, 2))
    wet_pad = jnp.pad(ocean_indicator, spread)
    east_faces = jnp.pad(zonal_boundary_transport, spread)[:, 1:grid_x + 2, 2:grid_y + 2]
    north_faces = jnp.pad(meridional_boundary_transport, spread)[:, 2:grid_x + 2, 1:grid_y + 2]

    def advect_tracer(tracer):
        conc_pad = jnp.pad(tracer * ocean_indicator, spread)[None]
        return advect(conc_pad, wet_pad, east_faces, north_faces)[0]

    moved = lax.map(advect_tracer, solute_amounts)
    blended_solutes = diffuse(moved, diffusion_factor, ocean_indicator)
    advanced_solutes = perform_chemistry(blended_solutes, thermal_state, saltiness_field, chemistry_matrix, ocean_indicator)
    absorption = ocean_indicator * (0.02 + 0.04 * jnp.maximum(advanced_solutes[0], 0.0))
    optical_depth = jnp.cumsum(absorption, 0) - absorption
    heating = 16.0 * jnp.exp(-optical_depth) * (1.0 - jnp.exp(-absorption))
    return advanced_solutes, heating
```

```python
import jax
import jax.numpy as jnp
from jax import lax
from jax.experimental import pallas as pl
from jax.experimental.pallas import tpu as pltpu
from jax.sharding import PartitionSpec as P

NTR = 19
LEV = 16
LANES = 128
BLOCK = 2 * LEV
ROWS = 12
EAST_LOW, EAST, NORTH, EDGE_LOW, EDGE_HIGH, KAPPA, GROWTH = 0, 1, 3, 5, 6, 7, 9


def lane_index():
    return lax.broadcasted_iota(jnp.int32, (LEV, LANES), 1)


def row_index():
    return lax.broadcasted_iota(jnp.int32, (LEV, LANES), 0)


def rows(ref, start, stride):
    return ref[pl.ds(start, LEV, stride=stride), :]


def minmod(first, second):
    return jnp.maximum(jnp.minimum(first, second), 0.0) + jnp.minimum(
        jnp.maximum(first, second), 0.0
    )


def pack_fields(east, north, kappa, temp, salt, north_left, out):
    def put(place, value):
        out[pl.ds(place, LEV, stride=ROWS), :] = value

    put(ROWS - 1, jnp.zeros((LEV, LANES), jnp.float32))
    low_half = lane_index() < LANES // 2
    even, odd = (rows(east, 0, 2), rows(east, 1, 2))
    put(EAST_LOW, jnp.where(row_index() == 0, 0.0, pltpu.roll(odd, 1, 0)))
    put(EAST, even)
    put(EAST + 1, odd)
    for place, source in ((EDGE_LOW, north_left), (EDGE_HIGH, north)):
        pair = [rows(source, i, 2)[:, LANES - 1 :] for i in range(2)]
        put(place, jnp.where(low_half, pair[0], pair[1]))
    for i in range(2):
        put(NORTH + i, rows(north, i, 2))
        put(KAPPA + i, rows(kappa, i, 2))
        growth = jnp.exp(0.0633 * (rows(temp, i, 2) - 15.0)) * (
            1.0 + 0.25 * (rows(salt, i, 2) - 35.0)
        )
        put(GROWTH + i, growth)


def wet_masks(tally):
    level = row_index()
    return [level < tally[i : i + 1, :] for i in range(2)]


def mask_and_edges(amounts, tally, conc, first, last):
    lane = lane_index()
    wet = wet_masks(tally)
    low, high = (jnp.zeros((LEV, LANES), jnp.float32), jnp.zeros((LEV, LANES), jnp.float32))
    for t in range(NTR):
        for i in range(2):
            value = jnp.where(wet[i], rows(amounts, t * BLOCK + i, 2), 0.0)
            conc[t * BLOCK + i * LEV : t * BLOCK + (i + 1) * LEV, :] = value
            place = 64 * i + 2 * t
            here = (lane == place) | (lane == place + 1)
            low = jnp.where(here, pltpu.roll(value, place, 1) if place else value, low)
            high = jnp.where(here, pltpu.roll(value, place + 2, 1), high)
    first[...] = low
    last[...] = high


def face(courant):
    positive = courant >= 0
    weight = jnp.where(positive, 0.5 * (1.0 - courant), -0.5 * (1.0 + courant))
    return courant, positive, weight


def flux(edge, low, high, slope_low, slope_high):
    courant, positive, weight = edge
    return courant * (
        jnp.where(positive, low, high) + weight * jnp.where(positive, slope_low, slope_high)
    )


def advect_and_heat(
    chem, conc, below, above, left, right, own_first, own_last, fields, tally,
    moved, heat, ratios, inverses, links, couple, source, answer,
):
    lane = lane_index()
    level = row_index()
    wet = wet_masks(tally)
    wet_f = [w.astype(jnp.float32) for w in wet]
    wet_below = (below[LEV : 2 * LEV, :] > 0).astype(jnp.float32)
    wet_above = (above[0:LEV, :] > 0).astype(jnp.float32)

    def field(place):
        return rows(fields, place, ROWS)

    x_faces = [
        face(field(EAST_LOW) * wet_below * wet_f[0]),
        face(field(EAST) * wet_f[0] * wet_f[1]),
        face(field(EAST + 1) * wet_f[1] * wet_above),
    ]
    at_last, at_first = (lane == LANES - 1, lane == 0)
    y_faces = []
    for i in range(2):
        y_faces.append(face(field(NORTH + i) * wet_f[i] * pltpu.roll(wet_f[i], LANES - 1, 1)))

    def second(packed):
        return pltpu.roll(packed, LANES - 1, 1)

    def edge_flux(courant, lower, upper):
        far_low, near_low = (lower, second(lower))
        near_high, far_high = (upper, second(upper))
        step_low, step, step_high = (near_low - far_low, near_high - near_low, far_high - near_high)
        open_face = ((near_low > 0) & (near_high > 0)).astype(jnp.float32)
        return (
            flux(
                face(courant * open_face), near_low, near_high,
                minmod(step_low, step), minmod(step, step_high),
            ),
            step,
        )

    flux_first, step_first = edge_flux(field(EDGE_LOW), left[...], own_first[...])
    flux_last, unused = edge_flux(field(EDGE_HIGH), own_last[...], right[...])
    odd_lane = lane % 2 == 1
    patch_steps = jnp.where(odd_lane, pltpu.roll(right[...], 1, 1), step_first)
    patch_flux = jnp.where(odd_lane, pltpu.roll(flux_first, 1, 1), flux_last)

    mixture = [jnp.zeros((LEV, LANES), jnp.float32) for i in range(2)]
    for t in range(NTR):
        base = t * BLOCK
        far_low, near_low = (below[base : base + LEV, :], below[base + LEV : base + BLOCK, :])
        cells = [conc[base : base + LEV, :], conc[base + LEV : base + BLOCK, :]]
        near_high, far_high = (above[base : base + LEV, :], above[base + LEV : base + BLOCK, :])
        line = [far_low, near_low, cells[0], cells[1], near_high, far_high]
        steps = [line[n + 1] - line[n] for n in range(5)]
        slopes = [minmod(steps[n], steps[n + 1]) for n in range(4)]
        x_flux = [
            flux(x_faces[n], line[n + 1], line[n + 2], slopes[n], slopes[n + 1]) for n in range(3)
        ]
        weight = chem[0, t]
        for i in range(2):
            here = cells[i]
            turn = (LANES - (64 * i + 2 * t) - 1) % LANES
            steps_patch = pltpu.roll(patch_steps, turn, 1) if turn else patch_steps
            flux_patch = pltpu.roll(patch_flux, turn, 1) if turn else patch_flux
            following = pltpu.roll(jnp.where(at_first, steps_patch, here), LANES - 1, 1)
            step = following - here
            step_before = pltpu.roll(jnp.where(at_last, steps_patch, step), 1, 1)
            slope = minmod(step_before, step)
            upper = flux(y_faces[i], here, following, slope, pltpu.roll(slope, LANES - 1, 1))
            upper = jnp.where(at_last, flux_patch, upper)
            lower = jnp.where(at_first, flux_patch, pltpu.roll(upper, 1, 1))
            value = here + (x_flux[i] - x_flux[i + 1]) + (lower - upper)
            moved[base + i * LEV : base + (i + 1) * LEV, :] = value
            mixture[i] = mixture[i] + weight * value

    for i in range(2):
        next_wet = jnp.where(level == LEV - 1, 0.0, pltpu.roll(wet_f[i], LEV - 1, 0))
        coupling = field(KAPPA + i) * wet_f[i] * next_wet
        for r in range(i, 8, 2):
            couple[pl.ds(r, LEV, stride=8), :] = coupling
            source[pl.ds(r, LEV, stride=8), :] = (
                moved[i * LEV : (i + 1) * LEV, :] if r < 2 else mixture[i]
            )
    zero = jnp.zeros((8, LANES), jnp.float32)
    upper_link, ratio, carried = (zero, zero, zero)
    for k in range(LEV):
        at = slice(8 * k, 8 * k + 8)
        coupling = couple[at, :]
        inverse = 1.0 / (1.0 + upper_link + coupling + upper_link * ratio)
        ratio = -coupling * inverse
        carried = (source[at, :] + upper_link * carried) * inverse
        ratios[at, :] = ratio
        inverses[at, :] = inverse
        links[at, :] = upper_link * inverse
        answer[at, :] = carried
        upper_link = coupling
    solved = zero
    for k in reversed(range(LEV)):
        at = slice(8 * k, 8 * k + 8)
        solved = answer[at, :] - ratios[at, :] * solved
        answer[at, :] = solved
    for i in range(2):
        tracer, mixed = (rows(answer, i, 8), rows(answer, 2 + i, 8))
        advanced = tracer + 0.2 * field(GROWTH + i) * mixed
        absorption = jnp.where(wet[i], 0.02 + 0.04 * jnp.maximum(advanced, 0.0), 0.0)
        depth = absorption
        for shift in (1, 2, 4, 8):
            depth = depth + jnp.where(level >= shift, pltpu.roll(depth, shift, 0), 0.0)
        depth = depth - absorption
        heat[pl.ds(i, LEV, stride=2), :] = (
            16.0 * jnp.exp(-depth) * (1.0 - jnp.exp(-absorption))
        )


def mix_and_react(chem, moved, ratios, inverses, links, fields, tally, out, work, rate):
    shape = (NTR, LANES)
    wet = wet_masks(tally)
    for i in range(2):
        carried = jnp.zeros(shape, jnp.float32)
        for k in range(LEV):
            row = slice(8 * k + i, 8 * k + i + 1)
            at = pl.ds(i * LEV + k, NTR, stride=BLOCK)
            carried = moved[at, :] * inverses[row, :] + links[row, :] * carried
            work[at, :] = carried
        solved = jnp.zeros(shape, jnp.float32)
        for k in reversed(range(LEV)):
            row = slice(8 * k + i, 8 * k + i + 1)
            at = pl.ds(i * LEV + k, NTR, stride=BLOCK)
            solved = work[at, :] - ratios[row, :] * solved
            work[at, :] = solved
        rate[i * LEV : (i + 1) * LEV, :] = 0.2 * rows(fields, GROWTH + i, ROWS)
    for i in range(2):
        for half in range(2):
            start = i * LEV + 8 * half
            values = [work[t * BLOCK + start : t * BLOCK + start + 8, :] for t in range(NTR)]
            speed = rate[start : start + 8, :]
            is_wet = wet[i][8 * half : 8 * half + 8, :]
            for t in range(NTR):
                total = chem[t, 0] * values[0]
                for j in range(1, NTR):
                    total = total + chem[t, j] * values[j]
                out[pl.ds(t * BLOCK + 16 * half + i, 8, stride=2), :] = jnp.where(
                    is_wet, values[t] + speed * total, 0.0
                )


def shape_of(count):
    return pltpu.VMEM((count, LANES), jnp.float32)


def body(
    solute_amounts,
    submerged_layer_tally,
    zonal_boundary_transport,
    meridional_boundary_transport,
    diffusion_factor,
    thermal_state,
    saltiness_field,
    chemistry_matrix,
):
    sects = lax.axis_size("sect")
    across = ("tx", "ty")
    strips = lax.axis_size(across)
    smem = pl.BlockSpec(memory_space=pltpu.SMEM)
    vmem = pl.BlockSpec(memory_space=pltpu.VMEM)

    def upward(array, axis, count):
        return lax.ppermute(array, axis, [(n, n + 1) for n in range(count - 1)])

    def downward(array, axis, count):
        return lax.ppermute(array, axis, [(n + 1, n) for n in range(count - 1)])

    def flat(array):
        return array.reshape(-1, LANES)

    def near(*arrays):
        return [pltpu.with_memory_space_constraint(array, pltpu.VMEM) for array in arrays]

    north = flat(meridional_boundary_transport)
    north_left = upward(north, across, strips)
    sent = pl.pallas_call(pack_fields, out_shape=shape_of(LEV * ROWS), name="pack_fields")(
        flat(zonal_boundary_transport), north, flat(diffusion_factor), flat(thermal_state),
        flat(saltiness_field), *near(north_left),
    )
    fields = flat(
        lax.all_to_all(
            sent.reshape(LEV, ROWS // 4, 4, LANES), "sect", split_axis=0, concat_axis=0, tiled=True
        )
    )
    conc, first, last = pl.pallas_call(
        mask_and_edges,
        out_shape=(shape_of(NTR * BLOCK), shape_of(LEV), shape_of(LEV)),
        name="mask_and_edges",
    )(*near(flat(solute_amounts), submerged_layer_tally))
    below = upward(conc, "sect", sects)
    above = downward(conc, "sect", sects)
    left = upward(last, across, strips)
    right = downward(first, across, strips)
    column = shape_of(8 * LEV)
    moved, heat, ratios, inverses, links = pl.pallas_call(
        advect_and_heat,
        out_shape=(shape_of(NTR * BLOCK), shape_of(BLOCK), column, column, column),
        in_specs=[smem] + [vmem] * 9,
        scratch_shapes=[pltpu.VMEM((8 * LEV, LANES), jnp.float32)] * 3,
        name="advect_and_heat",
    )(
        chemistry_matrix,
        *near(
            conc, below, above, left, right, first, last, fields, submerged_layer_tally
        ),
    )
    heating = lax.all_to_all(heat, "sect", split_axis=0, concat_axis=0, tiled=True)
    advanced = pl.pallas_call(
        mix_and_react,
        out_shape=jax.ShapeDtypeStruct((NTR * BLOCK, LANES), jnp.float32),
        in_specs=[smem] + [vmem] * 6,
        scratch_shapes=[
            pltpu.VMEM((NTR * BLOCK, LANES), jnp.float32),
            pltpu.VMEM((BLOCK, LANES), jnp.float32),
        ],
        name="mix_and_react",
    )(
        chemistry_matrix,
        *near(moved, ratios, inverses, links, fields, submerged_layer_tally),
    )
    return (
        advanced.reshape(solute_amounts.shape),
        heating.reshape(zonal_boundary_transport.shape),
    )


def solution(mesh):
    in_specs = (
        P(None, None, "sect", ("tx", "ty")),
        P("sect", ("tx", "ty")),
        P("sect", None, ("tx", "ty")),
        P("sect", None, ("tx", "ty")),
        P("sect", None, ("tx", "ty")),
        P("sect", None, ("tx", "ty")),
        P("sect", None, ("tx", "ty")),
        P(),
    )
    out_specs = (P(None, None, "sect", ("tx", "ty")), P("sect", None, ("tx", "ty")))
    return jax.shard_map(body, mesh=mesh, in_specs=in_specs, out_specs=out_specs, check_vma=False)
```

```python
import jax
import jax.numpy as jnp
from jax import lax
from jax.experimental import pallas as pl
from jax.experimental.pallas import tpu as pltpu
from jax.sharding import PartitionSpec as P


NTR = 19
LEV = 16
LANES = 128
BLOCK = 2 * LEV
ROWS = 12
EAST_LOW, EAST, NORTH, EDGE_LOW, EDGE_HIGH, KAPPA, GROWTH = 0, 1, 3, 5, 6, 7, 9
FIELD_ROOT = 12
HEAT_ROOT = 8


def lane_index():
    return lax.broadcasted_iota(jnp.int32, (LEV, LANES), 1)


def row_index():
    return lax.broadcasted_iota(jnp.int32, (LEV, LANES), 0)


def rows(ref, start, stride):
    return ref[pl.ds(start, LEV, stride=stride), :]


def rotate(value, root):
    return pltpu.roll(value, (LEV - root) % LEV, 0) if root % LEV else value


def minmod(first, second):
    return jnp.maximum(jnp.minimum(first, second), 0.0) + jnp.minimum(
        jnp.maximum(first, second), 0.0
    )


def prepare(
    amounts, tally, east, north, kappa, temp, salt, conc, sent, near_swap, far_swap, first, last, wet
):
    def put(place, value):
        sent[pl.ds(place, LEV, stride=ROWS), :] = rotate(value, FIELD_ROOT)

    lane = lane_index()
    level = row_index()
    even, odd = (rows(east, 0, 2), rows(east, 1, 2))
    put(EAST_LOW, jnp.where(level == 0, 0.0, pltpu.roll(odd, 1, 0)))
    put(EAST, even)
    put(EAST + 1, odd)
    pair = [rows(north, i, 2)[:, LANES - 1 :] for i in range(2)]
    edge = jnp.where(lane < LANES // 2, pair[0], pair[1])
    put(EDGE_HIGH, edge)
    for place in (EDGE_LOW, ROWS - 1):
        put(place, jnp.zeros((LEV, LANES), jnp.float32))
    for i in range(2):
        put(NORTH + i, rows(north, i, 2))
        put(KAPPA + i, rows(kappa, i, 2))
        growth = jnp.exp(0.0633 * (rows(temp, i, 2) - 15.0)) * (
            1.0 + 0.25 * (rows(salt, i, 2) - 35.0)
        )
        put(GROWTH + i, growth)
    is_wet = [level < tally[i : i + 1, :] for i in range(2)]
    low, high = (jnp.zeros((LEV, LANES), jnp.float32), jnp.zeros((LEV, LANES), jnp.float32))
    for t in range(NTR):
        for i in range(2):
            value = jnp.where(is_wet[i], rows(amounts, t * BLOCK + i, 2), 0.0)
            conc[t * BLOCK + i * LEV : t * BLOCK + (i + 1) * LEV, :] = value
            place = 64 * i + 2 * t
            here = (lane == place) | (lane == place + 1)
            low = jnp.where(here, pltpu.roll(value, place, 1) if place else value, low)
            high = jnp.where(here, pltpu.roll(value, place + 2, 1), high)
    first[...] = low
    last[...] = high
    for i in range(2):
        wet[i * LEV : (i + 1) * LEV, :] = is_wet[i].astype(jnp.float32)
    is_even = even_strip()
    near_swap[:LEV, :] = jnp.where(is_even, high, low)
    near_swap[LEV:, :] = edge
    far_swap[:LEV, :] = jnp.where(is_even, low, high)
    far_swap[LEV:, :] = edge


def even_strip():
    return lax.axis_index("ty") % 2 == 0


def from_left(near_got, far_got, part):
    return jnp.where(even_strip(), far_got[part, :], near_got[part, :])


def from_right(near_got, far_got, part):
    return jnp.where(even_strip(), near_got[part, :], far_got[part, :])


def add_left_edge(sent, near_got, far_got, out):
    out[...] = sent[...]
    edge = from_left(near_got, far_got, slice(LEV, 2 * LEV))
    out[pl.ds(EDGE_LOW, LEV, stride=ROWS), :] = rotate(edge, FIELD_ROOT)


def face(courant):
    positive = courant >= 0
    weight = jnp.where(positive, 0.5 * (1.0 - courant), -0.5 * (1.0 + courant))
    return courant, positive, weight


def flux(edge, low, high, slope_low, slope_high):
    courant, positive, weight = edge
    return courant * (
        jnp.where(positive, low, high) + weight * jnp.where(positive, slope_low, slope_high)
    )


def advect_and_heat(
    chem, conc, below, above, near_got, far_got, own_first, own_last, fields, wet,
    moved, heat, ratios, inverses, links, rate, couple, source, answer,
):
    lane = lane_index()
    level = row_index()
    wet_f = [wet[i * LEV : (i + 1) * LEV, :] for i in range(2)]
    left = from_left(near_got, far_got, slice(0, LEV))
    right = from_right(near_got, far_got, slice(0, LEV))
    wet_below = (below[LEV : 2 * LEV, :] > 0).astype(jnp.float32)
    wet_above = (above[0:LEV, :] > 0).astype(jnp.float32)

    def field(place):
        return rotate(rows(fields, place, ROWS), LEV - FIELD_ROOT)

    x_faces = [
        face(field(EAST_LOW) * wet_below * wet_f[0]),
        face(field(EAST) * wet_f[0] * wet_f[1]),
        face(field(EAST + 1) * wet_f[1] * wet_above),
    ]
    at_last, at_first = (lane == LANES - 1, lane == 0)
    y_faces = []
    for i in range(2):
        y_faces.append(face(field(NORTH + i) * wet_f[i] * pltpu.roll(wet_f[i], LANES - 1, 1)))

    def second(packed):
        return pltpu.roll(packed, LANES - 1, 1)

    def edge_flux(courant, lower, upper):
        far_low, near_low = (lower, second(lower))
        near_high, far_high = (upper, second(upper))
        step_low, step, step_high = (near_low - far_low, near_high - near_low, far_high - near_high)
        open_face = ((near_low > 0) & (near_high > 0)).astype(jnp.float32)
        return (
            flux(
                face(courant * open_face), near_low, near_high,
                minmod(step_low, step), minmod(step, step_high),
            ),
            step,
        )

    flux_first, step_first = edge_flux(field(EDGE_LOW), left, own_first[...])
    flux_last, _ = edge_flux(field(EDGE_HIGH), own_last[...], right)
    odd_lane = lane % 2 == 1
    patch_steps = jnp.where(odd_lane, pltpu.roll(right, 1, 1), step_first)
    patch_flux = jnp.where(odd_lane, pltpu.roll(flux_first, 1, 1), flux_last)

    mixture = [jnp.zeros((LEV, LANES), jnp.float32) for _ in range(2)]
    for t in range(NTR):
        base = t * BLOCK
        far_low, near_low = (below[base : base + LEV, :], below[base + LEV : base + BLOCK, :])
        cells = [conc[base : base + LEV, :], conc[base + LEV : base + BLOCK, :]]
        near_high, far_high = (above[base : base + LEV, :], above[base + LEV : base + BLOCK, :])
        line = [far_low, near_low, cells[0], cells[1], near_high, far_high]
        steps = [line[n + 1] - line[n] for n in range(5)]
        slopes = [minmod(steps[n], steps[n + 1]) for n in range(4)]
        x_flux = [
            flux(x_faces[n], line[n + 1], line[n + 2], slopes[n], slopes[n + 1]) for n in range(3)
        ]
        weight = chem[0, t]
        for i in range(2):
            here = cells[i]
            turn = (LANES - (64 * i + 2 * t) - 1) % LANES
            steps_patch = pltpu.roll(patch_steps, turn, 1) if turn else patch_steps
            flux_patch = pltpu.roll(patch_flux, turn, 1) if turn else patch_flux
            following = pltpu.roll(jnp.where(at_first, steps_patch, here), LANES - 1, 1)
            step = following - here
            step_before = pltpu.roll(jnp.where(at_last, steps_patch, step), 1, 1)
            slope = minmod(step_before, step)
            upper = flux(y_faces[i], here, following, slope, pltpu.roll(slope, LANES - 1, 1))
            upper = jnp.where(at_last, flux_patch, upper)
            lower = jnp.where(at_first, flux_patch, pltpu.roll(upper, 1, 1))
            value = here + (x_flux[i] - x_flux[i + 1]) + (lower - upper)
            moved[base + i * LEV : base + (i + 1) * LEV, :] = value
            mixture[i] = mixture[i] + weight * value

    for i in range(2):
        next_wet = jnp.where(level == LEV - 1, 0.0, pltpu.roll(wet_f[i], LEV - 1, 0))
        coupling = field(KAPPA + i) * wet_f[i] * next_wet
        for r in range(i, 8, 2):
            couple[pl.ds(r, LEV, stride=8), :] = coupling
            source[pl.ds(r, LEV, stride=8), :] = (
                moved[i * LEV : (i + 1) * LEV, :] if r < 2 else mixture[i]
            )
    zero = jnp.zeros((8, LANES), jnp.float32)
    upper_link, ratio, carried = (zero, zero, zero)
    for k in range(LEV):
        at = slice(8 * k, 8 * k + 8)
        coupling = couple[at, :]
        inverse = 1.0 / (1.0 + upper_link + coupling + upper_link * ratio)
        ratio = -coupling * inverse
        carried = (source[at, :] + upper_link * carried) * inverse
        ratios[at, :] = ratio
        inverses[at, :] = inverse
        links[at, :] = upper_link * inverse
        answer[at, :] = carried
        upper_link = coupling
    solved = zero
    for k in reversed(range(LEV)):
        at = slice(8 * k, 8 * k + 8)
        solved = answer[at, :] - ratios[at, :] * solved
        answer[at, :] = solved
    for i in range(2):
        rate[i * LEV : (i + 1) * LEV, :] = 0.2 * field(GROWTH + i)
        tracer, mixed = (rows(answer, i, 8), rows(answer, 2 + i, 8))
        advanced = wet_f[i] * (tracer + rate[i * LEV : (i + 1) * LEV, :] * mixed)
        absorption = wet_f[i] * (0.02 + 0.04 * jnp.maximum(advanced, 0.0))
        depth = absorption
        for shift in (1, 2, 4, 8):
            depth = depth + jnp.where(level >= shift, pltpu.roll(depth, shift, 0), 0.0)
        depth = depth - absorption
        heat[pl.ds(i, LEV, stride=2), :] = rotate(
            16.0 * jnp.exp(-depth) * (1.0 - jnp.exp(-absorption)), HEAT_ROOT
        )


def mix_and_react(chem, moved, ratios, inverses, links, rate, wet, out, work):
    shape = (NTR, LANES)
    for i in range(2):
        carried = jnp.zeros(shape, jnp.float32)
        for k in range(LEV):
            row = slice(8 * k + i, 8 * k + i + 1)
            at = pl.ds(i * LEV + k, NTR, stride=BLOCK)
            carried = moved[at, :] * inverses[row, :] + links[row, :] * carried
            work[at, :] = carried
        solved = jnp.zeros(shape, jnp.float32)
        for k in reversed(range(LEV)):
            row = slice(8 * k + i, 8 * k + i + 1)
            at = pl.ds(i * LEV + k, NTR, stride=BLOCK)
            solved = work[at, :] - ratios[row, :] * solved
            work[at, :] = solved
    for i in range(2):
        for half in range(2):
            start = i * LEV + 8 * half
            values = [work[t * BLOCK + start : t * BLOCK + start + 8, :] for t in range(NTR)]
            speed = rate[start : start + 8, :]
            is_wet = wet[start : start + 8, :]
            for t in range(NTR):
                total = chem[t, 0] * values[0]
                for j in range(1, NTR):
                    total = total + chem[t, j] * values[j]
                out[pl.ds(t * BLOCK + 16 * half + i, 8, stride=2), :] = is_wet * (
                    values[t] + speed * total
                )


def shape_of(count):
    return pltpu.VMEM((count, LANES), jnp.float32)


def body(
    solute_amounts,
    submerged_layer_tally,
    zonal_boundary_transport,
    meridional_boundary_transport,
    diffusion_factor,
    thermal_state,
    saltiness_field,
    chemistry_matrix,
):
    sects = lax.axis_size("sect")
    across = ("tx", "ty")
    strips = lax.axis_size(across)
    smem = pl.BlockSpec(memory_space=pltpu.SMEM)
    vmem = pl.BlockSpec(memory_space=pltpu.VMEM)

    def upward(array, axis, count):
        return lax.ppermute(array, axis, [(n, n + 1) for n in range(count - 1)])

    def downward(array, axis, count):
        return lax.ppermute(array, axis, [(n + 1, n) for n in range(count - 1)])

    def flat(array):
        return array.reshape(-1, LANES)

    def near(*arrays):
        return [pltpu.with_memory_space_constraint(array, pltpu.VMEM) for array in arrays]

    def exchange(array, root):
        group = [(root + n) % sects for n in range(sects)]
        return lax.all_to_all(
            array, "sect", split_axis=0, concat_axis=0, tiled=True,
            axis_index_groups=[group] if root else None,
        )

    def swap(array, start):
        pairs = [(n, n + 1) for n in range(start, strips - 1, 2)]
        return lax.ppermute(array, across, pairs + [(high, low) for low, high in pairs])

    tile, half = (shape_of(NTR * BLOCK), shape_of(LEV))
    conc, sent, near_swap, far_swap, first, last, wet = pl.pallas_call(
        prepare,
        out_shape=(
            tile, shape_of(LEV * ROWS), shape_of(BLOCK), shape_of(BLOCK), half, half,
            shape_of(BLOCK),
        ),
        name="prepare",
    )(
        flat(solute_amounts), submerged_layer_tally, flat(zonal_boundary_transport),
        flat(meridional_boundary_transport), flat(diffusion_factor), flat(thermal_state),
        flat(saltiness_field),
    )
    far_got = swap(far_swap, 1)
    near_got = swap(near_swap, 0)
    below = upward(conc, "sect", sects)
    above = downward(conc, "sect", sects)
    sent = pl.pallas_call(
        add_left_edge,
        out_shape=jax.ShapeDtypeStruct((LEV * ROWS, LANES), jnp.float32),
        name="add_left_edge",
    )(*near(sent, near_got, far_got))
    fields = exchange(sent.reshape(LEV, ROWS // 4, 4, LANES), FIELD_ROOT)
    fields = flat(fields)
    column = shape_of(8 * LEV)
    moved, heat, ratios, inverses, links, rate = pl.pallas_call(
        advect_and_heat,
        out_shape=(tile, shape_of(BLOCK), column, column, column, shape_of(BLOCK)),
        in_specs=[smem] + [vmem] * 9,
        scratch_shapes=[pltpu.VMEM((8 * LEV, LANES), jnp.float32)] * 3,
        name="advect_and_heat",
    )(
        chemistry_matrix,
        *near(conc, below, above, near_got, far_got, first, last, fields, wet),
    )
    heating = flat(exchange(heat.reshape(LEV, 2, LANES), HEAT_ROOT))
    turn = 2 * HEAT_ROOT % BLOCK
    if turn:
        heating = jnp.concatenate([heating[BLOCK - turn :], heating[: BLOCK - turn]])
    advanced = pl.pallas_call(
        mix_and_react,
        out_shape=jax.ShapeDtypeStruct((NTR * BLOCK, LANES), jnp.float32),
        in_specs=[smem] + [vmem] * 6,
        scratch_shapes=[pltpu.VMEM((NTR * BLOCK, LANES), jnp.float32)],
        name="mix_and_react",
    )(chemistry_matrix, *near(moved, ratios, inverses, links, rate, wet))
    return (
        advanced.reshape(solute_amounts.shape),
        heating.reshape(zonal_boundary_transport.shape),
    )


def solution(mesh):
    in_specs = (
        P(None, None, "sect", ("tx", "ty")),
        P("sect", ("tx", "ty")),
        P("sect", None, ("tx", "ty")),
        P("sect", None, ("tx", "ty")),
        P("sect", None, ("tx", "ty")),
        P("sect", None, ("tx", "ty")),
        P("sect", None, ("tx", "ty")),
        P(),
    )
    out_specs = (P(None, None, "sect", ("tx", "ty")), P("sect", None, ("tx", "ty")))

    return jax.shard_map(body, mesh=mesh, in_specs=in_specs, out_specs=out_specs, check_vma=False)
```

```python
import jax
import jax.numpy as jnp
from jax import lax
from jax.experimental import pallas as pl
from jax.experimental.pallas import tpu as pltpu
from jax.sharding import PartitionSpec as P


NTR = 19
LEV = 16
LANES = 128
BLOCK = 2 * LEV
ROWS = 12
EAST_LOW, EAST, NORTH, EDGE_LOW, EDGE_HIGH, KAPPA, GROWTH = 0, 1, 3, 5, 6, 7, 9
FIELD_ROOT = 12
HEAT_ROOT = 8


def lane_index():
    return lax.broadcasted_iota(jnp.int32, (LEV, LANES), 1)


def row_index():
    return lax.broadcasted_iota(jnp.int32, (LEV, LANES), 0)


def rows(ref, start, stride):
    return ref[pl.ds(start, LEV, stride=stride), :]


def rotate(value, root):
    return pltpu.roll(value, (LEV - root) % LEV, 0) if root % LEV else value


def minmod(first, second):
    return jnp.maximum(
        jnp.minimum(first, second), jnp.minimum(jnp.maximum(first, second), 0.0)
    )


def prepare(
    amounts, tally, east, north, kappa, temp, salt, conc, sent, near_swap, far_swap, first, last, wet
):
    def put(place, value):
        sent[pl.ds(place, LEV, stride=ROWS), :] = rotate(value, FIELD_ROOT)

    lane = lane_index()
    level = row_index()
    even, odd = (rows(east, 0, 2), rows(east, 1, 2))
    put(EAST_LOW, jnp.where(level == 0, 0.0, pltpu.roll(odd, 1, 0)))
    put(EAST, even)
    put(EAST + 1, odd)
    pair = [rows(north, i, 2)[:, LANES - 1 :] for i in range(2)]
    edge = jnp.where(lane < LANES // 2, pair[0], pair[1])
    put(EDGE_HIGH, edge)
    for place in (EDGE_LOW, ROWS - 1):
        put(place, jnp.zeros((LEV, LANES), jnp.float32))
    for i in range(2):
        put(NORTH + i, rows(north, i, 2))
        put(KAPPA + i, rows(kappa, i, 2))
        growth = jnp.exp(0.0633 * (rows(temp, i, 2) - 15.0)) * (
            1.0 + 0.25 * (rows(salt, i, 2) - 35.0)
        )
        put(GROWTH + i, growth)
    is_wet = [level < tally[i : i + 1, :] for i in range(2)]
    low, high = (jnp.zeros((LEV, LANES), jnp.float32), jnp.zeros((LEV, LANES), jnp.float32))
    for t in range(NTR):
        for i in range(2):
            value = jnp.where(is_wet[i], rows(amounts, t * BLOCK + i, 2), 0.0)
            conc[t * BLOCK + i * LEV : t * BLOCK + (i + 1) * LEV, :] = value
            place = 64 * i + 2 * t
            here = (lane == place) | (lane == place + 1)
            low = jnp.where(here, pltpu.roll(value, place, 1) if place else value, low)
            high = jnp.where(here, pltpu.roll(value, place + 2, 1), high)
    first[...] = low
    last[...] = high
    for i in range(2):
        wet[i * LEV : (i + 1) * LEV, :] = is_wet[i].astype(jnp.float32)
    is_even = even_strip()
    near_swap[:LEV, :] = jnp.where(is_even, high, low)
    near_swap[LEV:, :] = edge
    far_swap[:LEV, :] = jnp.where(is_even, low, high)
    far_swap[LEV:, :] = edge


def even_strip():
    return lax.axis_index("ty") % 2 == 0


def from_left(near_got, far_got, part):
    return jnp.where(even_strip(), far_got[part, :], near_got[part, :])


def from_right(near_got, far_got, part):
    return jnp.where(even_strip(), near_got[part, :], far_got[part, :])


def add_left_edge(sent, near_got, far_got, out):
    out[...] = sent[...]
    edge = from_left(near_got, far_got, slice(LEV, 2 * LEV))
    out[pl.ds(EDGE_LOW, LEV, stride=ROWS), :] = rotate(edge, FIELD_ROOT)


def face(courant):
    positive = courant >= 0
    weight = jnp.where(positive, 0.5 * (1.0 - courant), -0.5 * (1.0 + courant))
    return courant, positive, weight


def flux(edge, low, high, slope_low, slope_high):
    courant, positive, weight = edge
    return courant * (
        jnp.where(positive, low, high) + weight * jnp.where(positive, slope_low, slope_high)
    )


def second(packed):
    return pltpu.roll(packed, LANES - 1, 1)


def to_ends(packed, place):
    turn = (LANES - place - 1) % LANES
    return pltpu.roll(packed, turn, 1) if turn else packed


def limit_slopes(
    conc, below, above, near_got, far_got, own_first, x_slopes, following, slopes, slopes_next
):
    lane = lane_index()
    at_last, at_first = (lane == LANES - 1, lane == 0)
    left = from_left(near_got, far_got, slice(0, LEV))
    right = from_right(near_got, far_got, slice(0, LEV))
    patch = jnp.where(lane % 2 == 1, pltpu.roll(right, 1, 1), own_first[...] - second(left))
    for t in range(NTR):
        halves = [slice(t * BLOCK + i * LEV, t * BLOCK + (i + 1) * LEV) for i in range(2)]
        line = [source[half, :] for source in (below, conc, above) for half in halves]
        steps = [line[n + 1] - line[n] for n in range(5)]
        for n in range(4):
            x_slopes[(4 * t + n) * LEV : (4 * t + n + 1) * LEV, :] = minmod(steps[n], steps[n + 1])
        for i in range(2):
            here = line[2 + i]
            ends = to_ends(patch, 64 * i + 2 * t)
            after = pltpu.roll(jnp.where(at_first, ends, here), LANES - 1, 1)
            step = after - here
            slope = minmod(pltpu.roll(jnp.where(at_last, ends, step), 1, 1), step)
            following[halves[i], :] = after
            slopes[halves[i], :] = slope
            slopes_next[halves[i], :] = pltpu.roll(slope, LANES - 1, 1)


def advect_and_heat(
    chem, conc, below, above, x_slopes, following, slopes, slopes_next,
    near_got, far_got, own_first, own_last, fields, wet,
    moved, heat, ratios, inverses, links, rate, couple, source, answer,
):
    lane = lane_index()
    level = row_index()
    wet_f = [wet[i * LEV : (i + 1) * LEV, :] for i in range(2)]
    left = from_left(near_got, far_got, slice(0, LEV))
    right = from_right(near_got, far_got, slice(0, LEV))
    wet_below = (below[LEV : 2 * LEV, :] > 0).astype(jnp.float32)
    wet_above = (above[0:LEV, :] > 0).astype(jnp.float32)

    def field(place):
        return rotate(rows(fields, place, ROWS), LEV - FIELD_ROOT)

    x_faces = [
        face(field(EAST_LOW) * wet_below * wet_f[0]),
        face(field(EAST) * wet_f[0] * wet_f[1]),
        face(field(EAST + 1) * wet_f[1] * wet_above),
    ]
    at_last, at_first = (lane == LANES - 1, lane == 0)
    y_faces = []
    for i in range(2):
        y_faces.append(face(field(NORTH + i) * wet_f[i] * pltpu.roll(wet_f[i], LANES - 1, 1)))

    def edge_flux(courant, lower, upper):
        far_low, near_low = (lower, second(lower))
        near_high, far_high = (upper, second(upper))
        step_low, step, step_high = (near_low - far_low, near_high - near_low, far_high - near_high)
        open_face = ((near_low > 0) & (near_high > 0)).astype(jnp.float32)
        return flux(
            face(courant * open_face), near_low, near_high,
            minmod(step_low, step), minmod(step, step_high),
        )

    flux_first = edge_flux(field(EDGE_LOW), left, own_first[...])
    flux_last = edge_flux(field(EDGE_HIGH), own_last[...], right)
    patch = jnp.where(lane % 2 == 1, pltpu.roll(flux_first, 1, 1), flux_last)

    for i in range(2):
        next_wet = jnp.where(level == LEV - 1, 0.0, pltpu.roll(wet_f[i], LEV - 1, 0))
        coupling = field(KAPPA + i) * wet_f[i] * next_wet
        for r in range(i, 8, 2):
            couple[pl.ds(r, LEV, stride=8), :] = coupling
    zero = jnp.zeros((8, LANES), jnp.float32)
    upper_link, ratio = (zero, zero)
    for k in range(LEV):
        at = slice(8 * k, 8 * k + 8)
        coupling = couple[at, :]
        inverse = 1.0 / (1.0 + upper_link + coupling + upper_link * ratio)
        ratio = -coupling * inverse
        ratios[at, :] = ratio
        inverses[at, :] = inverse
        links[at, :] = upper_link * inverse
        upper_link = coupling

    mixture = [jnp.zeros((LEV, LANES), jnp.float32) for _ in range(2)]
    for t in range(NTR):
        base = t * BLOCK
        halves = [slice(base + i * LEV, base + (i + 1) * LEV) for i in range(2)]
        line = [below[halves[1], :], conc[halves[0], :], conc[halves[1], :], above[halves[0], :]]
        x_slope = [x_slopes[(4 * t + n) * LEV : (4 * t + n + 1) * LEV, :] for n in range(4)]
        x_flux = [
            flux(x_faces[n], line[n], line[n + 1], x_slope[n], x_slope[n + 1]) for n in range(3)
        ]
        weight = chem[0:1, t : t + 1]
        for i in range(2):
            here = line[1 + i]
            half = halves[i]
            ends = to_ends(patch, 64 * i + 2 * t)
            upper = flux(
                y_faces[i], here, following[half, :], slopes[half, :], slopes_next[half, :]
            )
            upper = jnp.where(at_last, ends, upper)
            lower = jnp.where(at_first, ends, pltpu.roll(upper, 1, 1))
            value = here + (x_flux[i] - x_flux[i + 1]) + (lower - upper)
            moved[half, :] = value
            mixture[i] = mixture[i] + weight * value

    for i in range(2):
        for r in range(i, 8, 2):
            source[pl.ds(r, LEV, stride=8), :] = (
                moved[i * LEV : (i + 1) * LEV, :] if r < 2 else mixture[i]
            )
    carried = zero
    for k in range(LEV):
        at = slice(8 * k, 8 * k + 8)
        carried = source[at, :] * inverses[at, :] + links[at, :] * carried
        answer[at, :] = carried
    solved = zero
    for k in reversed(range(LEV)):
        at = slice(8 * k, 8 * k + 8)
        solved = answer[at, :] - ratios[at, :] * solved
        answer[at, :] = solved
    for i in range(2):
        rate[i * LEV : (i + 1) * LEV, :] = 0.2 * field(GROWTH + i)
        tracer, mixed = (rows(answer, i, 8), rows(answer, 2 + i, 8))
        advanced = wet_f[i] * (tracer + rate[i * LEV : (i + 1) * LEV, :] * mixed)
        absorption = wet_f[i] * (0.02 + 0.04 * jnp.maximum(advanced, 0.0))
        depth = absorption
        for shift in (1, 2, 4, 8):
            depth = depth + jnp.where(level >= shift, pltpu.roll(depth, shift, 0), 0.0)
        depth = depth - absorption
        heat[pl.ds(i, LEV, stride=2), :] = rotate(
            16.0 * jnp.exp(-depth) * (1.0 - jnp.exp(-absorption)), HEAT_ROOT
        )


def mix_and_react(chem, moved, ratios, inverses, links, rate, wet, out, work):
    pair = range(2)
    matrix = chem[...]

    def row(k, i):
        return slice(8 * k + i, 8 * k + i + 1)

    def place(k, i):
        return slice((2 * k + i) * BLOCK, (2 * k + i) * BLOCK + NTR)

    carried = [jnp.zeros((NTR, LANES), jnp.float32) for i in pair]
    for k in range(LEV):
        for i in pair:
            value = moved[pl.ds(i * LEV + k, NTR, stride=BLOCK), :]
            carried[i] = value * inverses[row(k, i), :] + links[row(k, i), :] * carried[i]
            work[place(k, i), :] = carried[i]
    solved = [jnp.zeros((NTR, LANES), jnp.float32) for i in pair]
    for k in reversed(range(LEV)):
        for i in pair:
            solved[i] = work[place(k, i), :] - ratios[row(k, i), :] * solved[i]
        reacted = jnp.dot(
            matrix, jnp.concatenate(solved, axis=1), precision=lax.Precision.HIGHEST,
            preferred_element_type=jnp.float32,
        )
        for i in pair:
            at = slice(i * LEV + k, i * LEV + k + 1)
            change = rate[at, :] * reacted[:, i * LANES : (i + 1) * LANES]
            out[pl.ds(2 * k + i, NTR, stride=BLOCK), :] = wet[at, :] * (solved[i] + change)


def shape_of(count):
    return pltpu.VMEM((count, LANES), jnp.float32)


def body(
    solute_amounts,
    submerged_layer_tally,
    zonal_boundary_transport,
    meridional_boundary_transport,
    diffusion_factor,
    thermal_state,
    saltiness_field,
    chemistry_matrix,
):
    sects = lax.axis_size("sect")
    across = ("tx", "ty")
    strips = lax.axis_size(across)
    vmem = pl.BlockSpec(memory_space=pltpu.VMEM)

    def upward(array, axis, count):
        return lax.ppermute(array, axis, [(n, n + 1) for n in range(count - 1)])

    def downward(array, axis, count):
        return lax.ppermute(array, axis, [(n + 1, n) for n in range(count - 1)])

    def flat(array):
        return array.reshape(-1, LANES)

    def near(*arrays):
        return [pltpu.with_memory_space_constraint(array, pltpu.VMEM) for array in arrays]

    def exchange(array, root):
        group = [(root + n) % sects for n in range(sects)]
        return lax.all_to_all(
            array, "sect", split_axis=0, concat_axis=0, tiled=True,
            axis_index_groups=[group] if root else None,
        )

    def swap(array, start):
        pairs = [(n, n + 1) for n in range(start, strips - 1, 2)]
        return lax.ppermute(array, across, pairs + [(high, low) for low, high in pairs])

    limits = pltpu.CompilerParams(vmem_limit_bytes=8 << 20)
    tile, half = (shape_of(NTR * BLOCK), shape_of(LEV))
    conc, sent, near_swap, far_swap, first, last, wet = pl.pallas_call(
        prepare,
        out_shape=(
            tile, shape_of(LEV * ROWS), shape_of(BLOCK), shape_of(BLOCK), half, half,
            shape_of(BLOCK),
        ),
        name="prepare",
    )(
        flat(solute_amounts), submerged_layer_tally, flat(zonal_boundary_transport),
        flat(meridional_boundary_transport), flat(diffusion_factor), flat(thermal_state),
        flat(saltiness_field),
    )
    far_got = swap(far_swap, 1)
    near_got = swap(near_swap, 0)
    below = upward(conc, "sect", sects)
    above = downward(conc, "sect", sects)
    sent = pl.pallas_call(
        add_left_edge,
        out_shape=jax.ShapeDtypeStruct((LEV * ROWS, LANES), jnp.float32),
        compiler_params=limits,
        name="add_left_edge",
    )(*near(sent, near_got, far_got))
    fields = exchange(sent.reshape(LEV, ROWS // 4, 4, LANES), FIELD_ROOT)
    fields = flat(fields)
    limited = pl.pallas_call(
        limit_slopes,
        out_shape=(shape_of(NTR * 4 * LEV), tile, tile, tile),
        compiler_params=limits,
        name="limit_slopes",
    )(*near(conc, below, above, near_got, far_got, first))
    column = shape_of(8 * LEV)
    moved, heat, ratios, inverses, links, rate = pl.pallas_call(
        advect_and_heat,
        out_shape=(tile, shape_of(BLOCK), column, column, column, shape_of(BLOCK)),
        in_specs=[vmem] * 14,
        scratch_shapes=[pltpu.VMEM((8 * LEV, LANES), jnp.float32)] * 3,
        compiler_params=limits,
        name="advect_and_heat",
    )(
        *near(
            chemistry_matrix, conc, below, above, *limited, near_got, far_got, first, last,
            fields, wet,
        ),
    )
    heating = flat(exchange(heat.reshape(LEV, 2, LANES), HEAT_ROOT))
    turn = 2 * HEAT_ROOT % BLOCK
    if turn:
        heating = jnp.concatenate([heating[BLOCK - turn :], heating[: BLOCK - turn]])
    advanced = pl.pallas_call(
        mix_and_react,
        out_shape=jax.ShapeDtypeStruct((NTR * BLOCK, LANES), jnp.float32),
        in_specs=[vmem] * 7,
        scratch_shapes=[pltpu.VMEM((BLOCK * BLOCK, LANES), jnp.float32)],
        compiler_params=limits,
        name="mix_and_react",
    )(*near(chemistry_matrix, moved, ratios, inverses, links, rate, wet))
    return (
        advanced.reshape(solute_amounts.shape),
        heating.reshape(zonal_boundary_transport.shape),
    )


def solution(mesh):
    in_specs = (
        P(None, None, "sect", ("tx", "ty")),
        P("sect", ("tx", "ty")),
        P("sect", None, ("tx", "ty")),
        P("sect", None, ("tx", "ty")),
        P("sect", None, ("tx", "ty")),
        P("sect", None, ("tx", "ty")),
        P("sect", None, ("tx", "ty")),
        P(),
    )
    out_specs = (P(None, None, "sect", ("tx", "ty")), P("sect", None, ("tx", "ty")))

    return jax.shard_map(body, mesh=mesh, in_specs=in_specs, out_specs=out_specs, check_vma=False)
```

```python
import jax
import jax.numpy as jnp
from jax import lax
from jax.experimental import pallas as pl
from jax.experimental.pallas import tpu as pltpu
from jax.sharding import PartitionSpec as P


NTR = 19
LEV = 16
LANES = 128
BLOCK = 2 * LEV
ROWS = 10
EAST_LOW, EAST, NORTH, EDGE_LOW, KAPPA, GROWTH = 0, 1, 3, 5, 6, 8
FIELD_ROOT = 11
HEAT_ROOT = 8


def lane_index():
    return lax.broadcasted_iota(jnp.int32, (LEV, LANES), 1)


def row_index():
    return lax.broadcasted_iota(jnp.int32, (LEV, LANES), 0)


def rows(ref, start, stride):
    return ref[pl.ds(start, LEV, stride=stride), :]


def rotate(value, root):
    return pltpu.roll(value, (LEV - root) % LEV, 0) if root % LEV else value


def minmod(first, second):
    return jnp.maximum(
        jnp.minimum(first, second), jnp.minimum(jnp.maximum(first, second), 0.0)
    )


def last_columns(pair):
    ends = [value[:, LANES - 1 :] for value in pair]
    return jnp.where(lane_index() < LANES // 2, ends[0], ends[1])


def prepare(
    amounts, tally, east, north, kappa, temp, salt, conc, sent, near_swap, far_swap, first, last, wet
):
    def put(place, value):
        sent[pl.ds(place, LEV, stride=ROWS), :] = rotate(value, FIELD_ROOT)

    lane = lane_index()
    level = row_index()
    even, odd = (rows(east, 0, 2), rows(east, 1, 2))
    put(EAST_LOW, jnp.where(level == 0, 0.0, pltpu.roll(odd, 1, 0)))
    put(EAST, even)
    put(EAST + 1, odd)
    edge = last_columns([rows(north, i, 2) for i in range(2)])
    put(EDGE_LOW, jnp.zeros((LEV, LANES), jnp.float32))
    for i in range(2):
        put(NORTH + i, rows(north, i, 2))
        put(KAPPA + i, rows(kappa, i, 2))
        growth = jnp.exp(0.0633 * (rows(temp, i, 2) - 15.0)) * (
            1.0 + 0.25 * (rows(salt, i, 2) - 35.0)
        )
        put(GROWTH + i, growth)
    is_wet = [level < tally[i : i + 1, :] for i in range(2)]
    low, high = (jnp.zeros((LEV, LANES), jnp.float32), jnp.zeros((LEV, LANES), jnp.float32))
    for t in range(NTR):
        for i in range(2):
            value = jnp.where(is_wet[i], rows(amounts, t * BLOCK + i, 2), 0.0)
            conc[t * BLOCK + i * LEV : t * BLOCK + (i + 1) * LEV, :] = value
            place = 64 * i + 2 * t
            here = (lane == place) | (lane == place + 1)
            low = jnp.where(here, pltpu.roll(value, place, 1) if place else value, low)
            high = jnp.where(here, pltpu.roll(value, place + 2, 1), high)
    first[...] = low
    last[...] = high
    for i in range(2):
        wet[i * LEV : (i + 1) * LEV, :] = is_wet[i].astype(jnp.float32)
    is_even = even_strip()
    near_swap[:LEV, :] = jnp.where(is_even, high, low)
    near_swap[LEV:, :] = edge
    far_swap[:LEV, :] = jnp.where(is_even, low, high)
    far_swap[LEV:, :] = edge


def even_strip():
    return lax.axis_index("ty") % 2 == 0


def from_left(near_got, far_got, part):
    return jnp.where(even_strip(), far_got[part, :], near_got[part, :])


def from_right(near_got, far_got, part):
    return jnp.where(even_strip(), near_got[part, :], far_got[part, :])


def add_left_edge(sent, near_got, far_got, out):
    out[...] = sent[...]
    edge = from_left(near_got, far_got, slice(LEV, 2 * LEV))
    out[pl.ds(EDGE_LOW, LEV, stride=ROWS), :] = rotate(edge, FIELD_ROOT)


def face(courant):
    positive = courant >= 0
    weight = jnp.where(positive, 0.5 * (1.0 - courant), -0.5 * (1.0 + courant))
    return courant, positive, weight


def flux(edge, low, high, slope_low, slope_high):
    courant, positive, weight = edge
    return courant * (
        jnp.where(positive, low, high) + weight * jnp.where(positive, slope_low, slope_high)
    )


def second(packed):
    return pltpu.roll(packed, LANES - 1, 1)


def to_ends(packed, place):
    turn = (LANES - place - 1) % LANES
    return pltpu.roll(packed, turn, 1) if turn else packed


def limit_slopes(
    conc, below, above, near_got, far_got, own_first, x_slopes, following, slopes, slopes_next
):
    lane = lane_index()
    at_last, at_first = (lane == LANES - 1, lane == 0)
    left = from_left(near_got, far_got, slice(0, LEV))
    right = from_right(near_got, far_got, slice(0, LEV))
    patch = jnp.where(lane % 2 == 1, pltpu.roll(right, 1, 1), own_first[...] - second(left))
    for t in range(NTR):
        halves = [slice(t * BLOCK + i * LEV, t * BLOCK + (i + 1) * LEV) for i in range(2)]
        line = [source[half, :] for source in (below, conc, above) for half in halves]
        steps = [line[n + 1] - line[n] for n in range(5)]
        for n in range(4):
            x_slopes[(4 * t + n) * LEV : (4 * t + n + 1) * LEV, :] = minmod(steps[n], steps[n + 1])
        for i in range(2):
            here = line[2 + i]
            ends = to_ends(patch, 64 * i + 2 * t)
            after = pltpu.roll(jnp.where(at_first, ends, here), LANES - 1, 1)
            step = after - here
            slope = minmod(pltpu.roll(jnp.where(at_last, ends, step), 1, 1), step)
            following[halves[i], :] = after
            slopes[halves[i], :] = slope
            slopes_next[halves[i], :] = pltpu.roll(slope, LANES - 1, 1)


def advect_and_heat(
    chem, conc, below, above, x_slopes, following, slopes, slopes_next,
    near_got, far_got, own_first, own_last, fields, wet,
    moved, heat, ratios, inverses, links, rate, couple, source, answer,
):
    lane = lane_index()
    level = row_index()
    wet_f = [wet[i * LEV : (i + 1) * LEV, :] for i in range(2)]
    left = from_left(near_got, far_got, slice(0, LEV))
    right = from_right(near_got, far_got, slice(0, LEV))
    wet_below = (below[LEV : 2 * LEV, :] > 0).astype(jnp.float32)
    wet_above = (above[0:LEV, :] > 0).astype(jnp.float32)

    def field(place):
        return rotate(rows(fields, place, ROWS), LEV - FIELD_ROOT)

    x_faces = [
        face(field(EAST_LOW) * wet_below * wet_f[0]),
        face(field(EAST) * wet_f[0] * wet_f[1]),
        face(field(EAST + 1) * wet_f[1] * wet_above),
    ]
    at_last, at_first = (lane == LANES - 1, lane == 0)
    y_faces = []
    for i in range(2):
        y_faces.append(face(field(NORTH + i) * wet_f[i] * pltpu.roll(wet_f[i], LANES - 1, 1)))

    def edge_flux(courant, lower, upper):
        far_low, near_low = (lower, second(lower))
        near_high, far_high = (upper, second(upper))
        step_low, step, step_high = (near_low - far_low, near_high - near_low, far_high - near_high)
        open_face = ((near_low > 0) & (near_high > 0)).astype(jnp.float32)
        return flux(
            face(courant * open_face), near_low, near_high,
            minmod(step_low, step), minmod(step, step_high),
        )

    flux_first = edge_flux(field(EDGE_LOW), left, own_first[...])
    flux_last = edge_flux(
        last_columns([field(NORTH), field(NORTH + 1)]), own_last[...], right
    )
    patch = jnp.where(lane % 2 == 1, pltpu.roll(flux_first, 1, 1), flux_last)

    for i in range(2):
        next_wet = jnp.where(level == LEV - 1, 0.0, pltpu.roll(wet_f[i], LEV - 1, 0))
        coupling = field(KAPPA + i) * wet_f[i] * next_wet
        for r in range(i, 8, 2):
            couple[pl.ds(r, LEV, stride=8), :] = coupling
    zero = jnp.zeros((8, LANES), jnp.float32)
    upper_link, ratio = (zero, zero)
    for k in range(LEV):
        at = slice(8 * k, 8 * k + 8)
        coupling = couple[at, :]
        inverse = 1.0 / (1.0 + upper_link + coupling + upper_link * ratio)
        ratio = -coupling * inverse
        ratios[at, :] = ratio
        inverses[at, :] = inverse
        links[at, :] = upper_link * inverse
        upper_link = coupling

    mixture = [jnp.zeros((LEV, LANES), jnp.float32) for _ in range(2)]
    for t in range(NTR):
        base = t * BLOCK
        halves = [slice(base + i * LEV, base + (i + 1) * LEV) for i in range(2)]
        line = [below[halves[1], :], conc[halves[0], :], conc[halves[1], :], above[halves[0], :]]
        x_slope = [x_slopes[(4 * t + n) * LEV : (4 * t + n + 1) * LEV, :] for n in range(4)]
        x_flux = [
            flux(x_faces[n], line[n], line[n + 1], x_slope[n], x_slope[n + 1]) for n in range(3)
        ]
        weight = chem[0:1, t : t + 1]
        for i in range(2):
            here = line[1 + i]
            half = halves[i]
            ends = to_ends(patch, 64 * i + 2 * t)
            upper = flux(
                y_faces[i], here, following[half, :], slopes[half, :], slopes_next[half, :]
            )
            upper = jnp.where(at_last, ends, upper)
            lower = jnp.where(at_first, ends, pltpu.roll(upper, 1, 1))
            value = here + (x_flux[i] - x_flux[i + 1]) + (lower - upper)
            moved[half, :] = value
            mixture[i] = mixture[i] + weight * value

    for i in range(2):
        for r in range(i, 8, 2):
            source[pl.ds(r, LEV, stride=8), :] = (
                moved[i * LEV : (i + 1) * LEV, :] if r < 2 else mixture[i]
            )
    carried = zero
    for k in range(LEV):
        at = slice(8 * k, 8 * k + 8)
        carried = source[at, :] * inverses[at, :] + links[at, :] * carried
        answer[at, :] = carried
    solved = zero
    for k in reversed(range(LEV)):
        at = slice(8 * k, 8 * k + 8)
        solved = answer[at, :] - ratios[at, :] * solved
        answer[at, :] = solved
    for i in range(2):
        rate[i * LEV : (i + 1) * LEV, :] = 0.2 * field(GROWTH + i)
        tracer, mixed = (rows(answer, i, 8), rows(answer, 2 + i, 8))
        advanced = wet_f[i] * (tracer + rate[i * LEV : (i + 1) * LEV, :] * mixed)
        absorption = wet_f[i] * (0.02 + 0.04 * jnp.maximum(advanced, 0.0))
        depth = absorption
        for shift in (1, 2, 4, 8):
            depth = depth + jnp.where(level >= shift, pltpu.roll(depth, shift, 0), 0.0)
        depth = depth - absorption
        heat[pl.ds(i, LEV, stride=2), :] = rotate(
            16.0 * jnp.exp(-depth) * (1.0 - jnp.exp(-absorption)), HEAT_ROOT
        )


def mix_and_react(chem, moved, ratios, inverses, links, rate, wet, out, work):
    pair = range(2)
    matrix = chem[...]

    def row(k, i):
        return slice(8 * k + i, 8 * k + i + 1)

    def place(k, i):
        return slice((2 * k + i) * BLOCK, (2 * k + i) * BLOCK + NTR)

    carried = [jnp.zeros((NTR, LANES), jnp.float32) for i in pair]
    for k in range(LEV):
        for i in pair:
            value = moved[pl.ds(i * LEV + k, NTR, stride=BLOCK), :]
            carried[i] = value * inverses[row(k, i), :] + links[row(k, i), :] * carried[i]
            work[place(k, i), :] = carried[i]
    solved = [jnp.zeros((NTR, LANES), jnp.float32) for i in pair]
    for k in reversed(range(LEV)):
        for i in pair:
            solved[i] = work[place(k, i), :] - ratios[row(k, i), :] * solved[i]
        reacted = jnp.dot(
            matrix, jnp.concatenate(solved, axis=1), precision=lax.Precision.HIGHEST,
            preferred_element_type=jnp.float32,
        )
        for i in pair:
            at = slice(i * LEV + k, i * LEV + k + 1)
            change = rate[at, :] * reacted[:, i * LANES : (i + 1) * LANES]
            out[pl.ds(2 * k + i, NTR, stride=BLOCK), :] = wet[at, :] * (solved[i] + change)


def shape_of(count):
    return pltpu.VMEM((count, LANES), jnp.float32)


def body(
    solute_amounts,
    submerged_layer_tally,
    zonal_boundary_transport,
    meridional_boundary_transport,
    diffusion_factor,
    thermal_state,
    saltiness_field,
    chemistry_matrix,
):
    sects = lax.axis_size("sect")
    across = ("tx", "ty")
    strips = lax.axis_size(across)
    vmem = pl.BlockSpec(memory_space=pltpu.VMEM)

    def upward(array, axis, count):
        return lax.ppermute(array, axis, [(n, n + 1) for n in range(count - 1)])

    def downward(array, axis, count):
        return lax.ppermute(array, axis, [(n + 1, n) for n in range(count - 1)])

    def flat(array):
        return array.reshape(-1, LANES)

    def near(*arrays):
        return [pltpu.with_memory_space_constraint(array, pltpu.VMEM) for array in arrays]

    def exchange(array, root):
        group = [(root + n) % sects for n in range(sects)]
        return lax.all_to_all(
            array, "sect", split_axis=0, concat_axis=0, tiled=True,
            axis_index_groups=[group] if root else None,
        )

    def swap(array, start):
        pairs = [(n, n + 1) for n in range(start, strips - 1, 2)]
        return lax.ppermute(array, across, pairs + [(high, low) for low, high in pairs])

    limits = pltpu.CompilerParams(vmem_limit_bytes=8 << 20)
    tile, half = (shape_of(NTR * BLOCK), shape_of(LEV))
    conc, sent, near_swap, far_swap, first, last, wet = pl.pallas_call(
        prepare,
        out_shape=(
            tile, shape_of(LEV * ROWS), shape_of(BLOCK), shape_of(BLOCK), half, half,
            shape_of(BLOCK),
        ),
        name="prepare",
    )(
        flat(solute_amounts), submerged_layer_tally, flat(zonal_boundary_transport),
        flat(meridional_boundary_transport), flat(diffusion_factor), flat(thermal_state),
        flat(saltiness_field),
    )
    far_got = swap(far_swap, 1)
    near_got = swap(near_swap, 0)
    below = upward(conc, "sect", sects)
    above = downward(conc, "sect", sects)
    sent = pl.pallas_call(
        add_left_edge,
        out_shape=jax.ShapeDtypeStruct((LEV * ROWS, LANES), jnp.float32),
        compiler_params=limits,
        name="add_left_edge",
    )(*near(sent, near_got, far_got))
    fields = exchange(sent.reshape(LEV, ROWS // 2, 2, LANES), FIELD_ROOT)
    fields = flat(fields)
    limited = pl.pallas_call(
        limit_slopes,
        out_shape=(shape_of(NTR * 4 * LEV), tile, tile, tile),
        compiler_params=limits,
        name="limit_slopes",
    )(*near(conc, below, above, near_got, far_got, first))
    column = shape_of(8 * LEV)
    moved, heat, ratios, inverses, links, rate = pl.pallas_call(
        advect_and_heat,
        out_shape=(tile, shape_of(BLOCK), column, column, column, shape_of(BLOCK)),
        in_specs=[vmem] * 14,
        scratch_shapes=[pltpu.VMEM((8 * LEV, LANES), jnp.float32)] * 3,
        compiler_params=limits,
        name="advect_and_heat",
    )(
        *near(
            chemistry_matrix, conc, below, above, *limited, near_got, far_got, first, last,
            fields, wet,
        ),
    )
    heating = flat(exchange(heat.reshape(LEV, 2, LANES), HEAT_ROOT))
    turn = 2 * HEAT_ROOT % BLOCK
    if turn:
        heating = jnp.concatenate([heating[BLOCK - turn :], heating[: BLOCK - turn]])
    advanced = pl.pallas_call(
        mix_and_react,
        out_shape=jax.ShapeDtypeStruct((NTR * BLOCK, LANES), jnp.float32),
        in_specs=[vmem] * 7,
        scratch_shapes=[pltpu.VMEM((BLOCK * BLOCK, LANES), jnp.float32)],
        compiler_params=limits,
        name="mix_and_react",
    )(*near(chemistry_matrix, moved, ratios, inverses, links, rate, wet))
    return (
        advanced.reshape(solute_amounts.shape),
        heating.reshape(zonal_boundary_transport.shape),
    )


def solution(mesh):
    in_specs = (
        P(None, None, "sect", ("tx", "ty")),
        P("sect", ("tx", "ty")),
        P("sect", None, ("tx", "ty")),
        P("sect", None, ("tx", "ty")),
        P("sect", None, ("tx", "ty")),
        P("sect", None, ("tx", "ty")),
        P("sect", None, ("tx", "ty")),
        P(),
    )
    out_specs = (P(None, None, "sect", ("tx", "ty")), P("sect", None, ("tx", "ty")))

    return jax.shard_map(body, mesh=mesh, in_specs=in_specs, out_specs=out_specs, check_vma=False)
```
